1024 devices in a mesh: dp: 16 (over y, x), expert: 32 (over z), tp: 2 (over core).
Axes of the slice: x: 4, y: 4, z: 32, core: 2. Of those that a mesh axis runs over, the one named last changes fastest.
Arguments:
- tokens: bfloat16 [8192, 2048], P(('dp', 'expert')), may hold values from -24 to 24
- grad_out: bfloat16 [8192, 2048], P(('dp', 'expert')), may hold values from -6 to 6
- expert_ids: int32 [8192, 8], P(('dp', 'expert')), may hold values from 0 to 31, all different within a row; in each aligned block of 16 rows (0 to 15, 16 to 31, ...) at most 6 rows name the same one
- route_probs: bfloat16 [8192, 8], P(('dp', 'expert')), may hold values from 0.049804688 to 1
- w_gate: bfloat16 [32, 2048, 768], P('expert', None, 'tp'), may hold values from -0.125 to 0.125
- w_up: bfloat16 [32, 2048, 768], P('expert', None, 'tp'), may hold values from -0.125 to 0.125
- w_down: bfloat16 [32, 768, 2048], P('expert', 'tp'), may hold values from -0.21875 to 0.21875
Outputs:
- d_tokens: bfloat16 [8192, 2048], P(('dp', 'expert'))
- d_probs: bfloat16 [8192, 8], P(('dp', 'expert'))
- grad_gate: bfloat16 [32, 2048, 768], P('expert', 'dp', 'tp')
- grad_up: bfloat16 [32, 2048, 768], P('expert', 'dp', 'tp')
- grad_down: bfloat16 [32, 768, 2048], P('expert', 'tp', 'dp')
The draws below stay inside these ranges and needn't reach their ends.
Inputs may be any that keep to these rules, and one draw needn't show every extreme that they name: `expert_ids`: each row names 8 different experts. At most 6 rows of one device's aligned block of 16 rows name one expert, and some block has exactly 6 rows naming one expert.
All inputs are finite; a program needn't handle non-finite values.
Results may differ from the reference program's by a relative error of at most 0.015.
Values may be sent and summed in bfloat16 or wider, within the bound.
No kernel may reach another device: no remote copies, remote signals or barrier semaphores. Data moves between devices by JAX's collectives and lax.ppermute only.
A program may use at most 64 MiB of HBM per device.

```python
import math
import jax
import jax.numpy as jnp
import numpy as np
from jax import lax

D = 2048
FF = 768
EXPERTS = 32
TOP = 8
TOK_DEV = 16
CAP = 6
TOKENS = 8192
N_DP = 16


def strengthened(array, key, source, target, shards_of, factor):
    owner, partner = [(jnp.arange(array.shape[position]) // (array.shape[position] // shards_of)).reshape([-1 if axis == position else 1 for axis in range(array.ndim)]) for position in (source, target)]
    chosen = jax.random.permutation(key, shards_of)[partner]
    strong = (owner == chosen) | (owner == (partner + shards_of // 2) % shards_of)
    return jnp.where(strong, factor * array, array)


def steps_of(rng, extent, shards, least, top_value):
    loudness = 1.0
    for position, parts in shards:
        draws = jax.random.uniform(jax.random.fold_in(jax.random.fold_in(rng, 6), position), (parts,), jnp.float32, least / len(shards), top_value / len(shards))
        loudness = loudness * jnp.repeat(jnp.exp(draws), extent[position] // parts).reshape((-1,) + (1,) * (len(extent) - 1 - position))
    return loudness


def deal_out(rng, own, number, rows, amount, top, most, lean):
    order = jax.random.permutation(rng, amount)
    heavy_load, ordinary = shares(amount, rows * top, most, lean, True), shares(amount, rows * top, most, lean, False)
    places = jnp.arange(amount)

    def named(tallies, turn):
        used = int((tallies > 0).sum())
        fixed = max(1, used // 4)
        shifted = fixed + (places - fixed + turn * (used - fixed)) % max(1, amount - fixed)
        return jnp.zeros((amount,), jnp.int32).at[order[jnp.where(places < fixed, places, shifted)]].set(jnp.asarray(tallies, jnp.int32))

    tallies = jnp.where(number % 4 == 0, named(heavy_load, number // 4), named(ordinary, number - number // 4 - 1))
    mixed = jax.random.permutation(jax.random.fold_in(own, 3), amount)
    source_of, taker = mixed[0:amount // 2 * 2:2], mixed[1:amount // 2 * 2:2]
    margin = jnp.minimum(tallies[source_of] - 1, most - tallies[taker]) // 2
    margin = jnp.where((source_of == order[0]) | (taker == order[0]) | (tallies[taker] == 0), 0, jnp.maximum(margin, 0))
    shifted = jax.random.randint(jax.random.fold_in(own, 4), (amount // 2,), 0, 1 << 20) % (margin + 1)
    tallies = tallies.at[source_of].add(-shifted).at[taker].add(shifted)
    members = jnp.searchsorted(jnp.cumsum(tallies), jnp.arange(rows * top), side="right").astype(jnp.int32)
    table = members.reshape(top, rows).T
    table = table[jax.random.permutation(jax.random.fold_in(own, 1), rows)]
    turn = jax.random.randint(jax.random.fold_in(own, 2), (rows, 1), 0, top)
    return jnp.take_along_axis(table, (jnp.arange(top)[None, :] + turn) % top, axis=1)


def shares(count, total, limit, slope, full):
    loads = [(1 << 20) // math.isqrt(rank ** slope) + 1 for rank in range(1, count + 1)]
    largest = limit if full else min(limit, max(-(-total // count), total * loads[0] // sum(loads)))
    least = 1 if total - largest >= count - 1 else 0
    counts, rest = [largest] + [least] * (count - 1), total - largest - least * (count - 1)
    while rest > 0:
        movable = [i for i in range(1, count) if counts[i] < largest] or [i for i in range(1, count) if counts[i] < limit]
        pool, left = sum([loads[i] for i in movable]), rest
        for i in movable:
            extra = min(limit - counts[i], max(1, left * loads[i] // pool), rest)
            counts[i] = counts[i] + extra
            rest = rest - extra
    return np.array(counts)


def bell_draw(stream_key, shape, spread, bound, pieces=(), kind=jnp.bfloat16):
    values = jax.random.normal(stream_key, shape, jnp.float32) * spread
    if len(pieces) > 0:
        values = steps_of(stream_key, shape, pieces, -0.22, 0.18) * values
    return jnp.clip(values, min=-bound, max=bound).astype(kind)


def gaussian_with(rng, dims, deviation, limit, shards, heavy, kind=jnp.bfloat16):
    entries = deviation * jax.random.normal(rng, dims, jnp.float32)
    if shards:
        entries = entries * steps_of(rng, dims, shards, -0.22, 0.18)
    return jnp.clip(strengthened(entries, jax.random.fold_in(rng, 3), *heavy), -limit, limit).astype(kind)


def setup_inputs(seed: int = 0) -> dict:
    arg_keys = jax.random.split(jax.random.key(seed), 8)
    tokens = gaussian_with(arg_keys[0], (TOKENS, D), 1.0, 24.0, ((0, 512),), (0, 1, 512, 6.0))
    grad_out = bell_draw(arg_keys[1], (TOKENS, D), 1.0, 6.0, ((0, 512),))
    expert_ids_keys = jax.random.split(jax.random.fold_in(arg_keys[2], 1), TOKENS // TOK_DEV)
    expert_ids_turns = jax.random.permutation(jax.random.fold_in(arg_keys[2], 3), TOKENS // TOK_DEV)
    expert_ids = jax.vmap(lambda own, number: deal_out(jax.random.fold_in(arg_keys[2], 2), own, number, TOK_DEV, EXPERTS, TOP, CAP, 2))(expert_ids_keys, expert_ids_turns).reshape((TOKENS, TOP))
    route_probs = jnp.clip(jnp.exp(math.log(1.0) - 2.9996462 * jax.random.uniform(arg_keys[3], (TOKENS, TOP), jnp.float32) ** steps_of(arg_keys[3], (TOKENS, TOP), ((0, 512),), -0.2, 0.2)), 0.049804688, 1.0).astype(jnp.bfloat16)
    w_gate = bell_draw(arg_keys[4], (EXPERTS, D, FF), D ** -0.5, 0.125, ((0, 32), (2, 2)))
    w_up = bell_draw(arg_keys[5], (EXPERTS, D, FF), D ** -0.5, 0.125, ((0, 32), (2, 2)))
    w_down = bell_draw(arg_keys[6], (EXPERTS, FF, D), FF ** -0.5, 0.21875, ((0, 32), (1, 2)))
    return dict(tokens=tokens, grad_out=grad_out, expert_ids=expert_ids, route_probs=route_probs, w_gate=w_gate, w_up=w_up, w_down=w_down)


def one_expert(inputs):
    x_rows, dy_rows, p_rows, gate_w, up_w, down_w = inputs
    gate = jnp.dot(x_rows, gate_w, preferred_element_type=jnp.float32)
    up = jnp.dot(x_rows, up_w, preferred_element_type=jnp.float32)
    silu_gate = jax.nn.silu(gate)
    hidden = (silu_gate * up).astype(jnp.bfloat16)
    back = jnp.dot(dy_rows, down_w.T, preferred_element_type=jnp.float32)
    prob_grad = jnp.sum(hidden.astype(jnp.float32) * back, axis=1).astype(jnp.bfloat16)
    weight = p_rows.astype(jnp.float32)[:, None]
    d_hidden = weight * back
    sigma = jax.nn.sigmoid(gate)
    d_gate = (d_hidden * up * sigma * (1.0 + gate * (1.0 - sigma))).astype(jnp.bfloat16)
    d_up = (d_hidden * silu_gate).astype(jnp.bfloat16)
    d_row = (jnp.dot(d_gate, gate_w.T, preferred_element_type=jnp.float32)
             + jnp.dot(d_up, up_w.T, preferred_element_type=jnp.float32)).astype(jnp.bfloat16)
    scaled = (weight * dy_rows.astype(jnp.float32)).astype(jnp.bfloat16)
    x_part = x_rows.astype(jnp.float32).reshape(N_DP, -1, D)
    y_part = scaled.astype(jnp.float32).reshape(N_DP, -1, D)
    h_part = hidden.astype(jnp.float32).reshape(N_DP, -1, FF)
    g_part = d_gate.astype(jnp.float32).reshape(N_DP, -1, FF)
    u_part = d_up.astype(jnp.float32).reshape(N_DP, -1, FF)
    gate_grad = jnp.einsum("nrd,nrf->ndf", x_part, g_part).astype(jnp.bfloat16)
    up_grad = jnp.einsum("nrd,nrf->ndf", x_part, u_part).astype(jnp.bfloat16)
    down_grad = jnp.einsum("nrf,nrd->nfd", h_part, y_part).astype(jnp.bfloat16)
    gate_grad = jnp.sum(gate_grad.astype(jnp.float32), axis=0).astype(jnp.bfloat16)
    up_grad = jnp.sum(up_grad.astype(jnp.float32), axis=0).astype(jnp.bfloat16)
    down_grad = jnp.sum(down_grad.astype(jnp.float32), axis=0).astype(jnp.bfloat16)
    return d_row, prob_grad, gate_grad, up_grad, down_grad


def reference(tokens, grad_out, expert_ids, route_probs, w_gate, w_up, w_down):
    blocks = TOKENS // TOK_DEV
    slot_count = TOK_DEV * TOP
    rows_all = blocks * CAP
    ids_block = expert_ids.reshape(blocks, slot_count)
    hits = (ids_block[:, :, None] == jnp.arange(EXPERTS, dtype=jnp.int32)[None, None, :]).astype(jnp.int32)
    earlier = jnp.cumsum(hits, axis=1) - hits
    rank = jnp.sum(earlier * hits, axis=2).astype(jnp.int32)
    dest_row = (jnp.arange(blocks, dtype=jnp.int32)[:, None] * CAP + rank).reshape(-1).astype(jnp.int32)
    dest_expert = expert_ids.reshape(-1).astype(jnp.int32)
    source_token = (jnp.arange(TOKENS * TOP, dtype=jnp.int32) // TOP).astype(jnp.int32)
    x_disp = jnp.zeros((EXPERTS, rows_all, D), jnp.bfloat16).at[dest_expert, dest_row].set(tokens[source_token])
    y_disp = jnp.zeros((EXPERTS, rows_all, D), jnp.bfloat16).at[dest_expert, dest_row].set(grad_out[source_token])
    p_disp = jnp.zeros((EXPERTS, rows_all), jnp.bfloat16).at[dest_expert, dest_row].set(route_probs.reshape(-1))
    d_disp, prob_disp, grad_gate, grad_up, grad_down = lax.map(
        one_expert, (x_disp, y_disp, p_disp, w_gate, w_up, w_down))
    picked = d_disp[dest_expert, dest_row].astype(jnp.float32).reshape(TOKENS, TOP, D)
    d_tokens = jnp.sum(picked, axis=1).astype(jnp.bfloat16)
    d_probs = prob_disp[dest_expert, dest_row].reshape(TOKENS, TOP)
    return d_tokens, d_probs, grad_gate, grad_up, grad_down
```

```python
import jax
import jax.numpy as jnp
from jax import lax
from jax.sharding import PartitionSpec as P

CAP = 6
ROWS = 8
F32 = jnp.float32
BF16 = jnp.bfloat16
SWAP = [(0, 1), (1, 0)]


def dot(a, b, ca, cb):
    return lax.dot_general(a, b, (((ca,), (cb,)), ((), ())), preferred_element_type=F32)


def local(tokens, grad_out, expert_ids, route_probs, w_gate, w_up, w_down):
    toks, width = tokens.shape
    top = expert_ids.shape[1]
    groups = lax.axis_size("expert")
    half = width // 2
    hidden_units = w_gate.shape[2]
    core = lax.axis_index("tp")
    first = core == 0
    wg, wu, wd = w_gate[0], w_up[0], w_down[0]

    n = toks * top
    slots = groups * ROWS
    flat = expert_ids.reshape(n)
    chosen = (flat[:, None] == lax.broadcasted_iota(jnp.int32, (n, groups), 1)).astype(BF16)
    lower = (
        lax.broadcasted_iota(jnp.int32, (n, n), 1) < lax.broadcasted_iota(jnp.int32, (n, n), 0)
    ).astype(BF16)
    rank = jnp.sum(dot(lower, chosen, 1, 0) * chosen.astype(F32), axis=1).astype(jnp.int32)
    placed = (flat * ROWS + rank)[:, None] == lax.broadcasted_iota(jnp.int32, (n, slots), 1)
    token_map = jnp.any(placed.reshape(toks, top, slots), axis=1).astype(BF16)

    x_half = jnp.where(first, tokens[:, :half], tokens[:, half:])
    dy_half = jnp.where(first, grad_out[:, :half], grad_out[:, half:])
    rows_sent = dot(token_map, jnp.concatenate([x_half, dy_half], axis=1), 0, 0).astype(BF16)
    at_rank = (rank[:, None] == lax.broadcasted_iota(jnp.int32, (n, 128), 1)).astype(F32)
    weight_at = (at_rank * route_probs.reshape(n, 1).astype(F32)).astype(BF16)
    weights_sent = dot(chosen, weight_at, 0, 0).astype(BF16)
    weights_sent = jnp.pad(weights_sent[:, None, :], ((0, 0), (0, 0), (0, 2 * half - 128)))
    spare = lax.broadcasted_iota(jnp.int32, (1, ROWS, 1), 1) == ROWS - 1
    sent = jnp.where(spare, weights_sent, rows_sent.reshape(groups, ROWS, 2 * half))
    recv = lax.all_to_all(sent, "expert", split_axis=0, concat_axis=0, tiled=True)
    weight = recv[:, ROWS - 1, :ROWS].astype(F32).reshape(slots, 1)
    used = lax.broadcasted_iota(jnp.int32, (slots, 1), 0) % ROWS < CAP
    weight = jnp.where(used, weight, 0.0)
    picked = jnp.where(used, recv.reshape(slots, 2 * half), jnp.zeros((), BF16))
    other = lax.ppermute(picked, "tp", SWAP)
    low, high = jnp.where(first, picked, other), jnp.where(first, other, picked)
    x = jnp.concatenate([low[:, :half], high[:, :half]], axis=1)
    dy = jnp.concatenate([low[:, half:], high[:, half:]], axis=1)

    gate = dot(x, wg, 1, 0)
    up = dot(x, wu, 1, 0)
    silu_gate = jax.nn.silu(gate)
    hidden = (silu_gate * up).astype(BF16)
    back = dot(dy, wd, 1, 1)
    prob_part = jnp.sum(hidden.astype(F32) * back, axis=1)
    d_hidden = weight * back
    sigma = jax.nn.sigmoid(gate)
    d_gate = (d_hidden * up * sigma * (1.0 + gate * (1.0 - sigma))).astype(BF16)
    d_up = (d_hidden * silu_gate).astype(BF16)
    row_part = dot(d_gate, wg, 1, 1) + dot(d_up, wu, 1, 1)
    scaled = (weight * dy.astype(F32)).astype(BF16)

    dp = lax.axis_size("dp")
    joined = jnp.concatenate(
        [
            dot(x, jnp.concatenate([d_gate, d_up], axis=1), 0, 0).astype(BF16),
            dot(scaled, hidden, 0, 0).astype(BF16),
        ],
        axis=1,
    )
    parts = lax.all_to_all(
        joined.reshape(dp, width // dp, 3 * hidden_units), "dp", split_axis=0, concat_axis=0,
        tiled=True,
    )
    grads = jnp.sum(parts.astype(F32), axis=0).astype(BF16)
    sums = [grads[:, i * hidden_units : (i + 1) * hidden_units] for i in range(3)]

    mine = jnp.where(first, row_part[:, :half], row_part[:, half:])
    yours = jnp.where(first, row_part[:, half:], row_part[:, :half])
    prob_pad = jnp.pad(prob_part.astype(BF16)[:, None], ((0, 0), (0, 127)))
    swapped = lax.ppermute(
        jnp.concatenate([yours.astype(BF16), prob_pad], axis=1), "tp", SWAP
    )
    d_row = (mine + swapped[:, :half].astype(F32)).astype(BF16)
    prob = (prob_part.astype(BF16).astype(F32) + swapped[:, half].astype(F32)).astype(BF16)
    prob_rows = prob.reshape(groups, ROWS)[:, None, :]
    prob_rows = jnp.pad(prob_rows, ((0, 0), (0, 0), (0, half - ROWS)))
    back_sent = jnp.where(spare, prob_rows, d_row.reshape(groups, ROWS, half))
    back_recv = lax.all_to_all(back_sent, "expert", split_axis=0, concat_axis=0, tiled=True)

    summed = dot(token_map, back_recv.reshape(slots, half), 1, 0).astype(BF16)
    summed_other = lax.ppermute(summed, "tp", SWAP)
    d_tokens = jnp.where(
        first,
        jnp.concatenate([summed, summed_other], axis=1),
        jnp.concatenate([summed_other, summed], axis=1),
    )
    prob_back = back_recv[:, ROWS - 1, :ROWS].astype(F32)
    by_expert = dot(chosen, prob_back.astype(BF16), 1, 0)
    rank_is = rank[:, None] == lax.broadcasted_iota(jnp.int32, (n, ROWS), 1)
    d_probs = jnp.sum(jnp.where(rank_is, by_expert, 0.0), axis=1).reshape(toks, top).astype(BF16)

    return (d_tokens, d_probs, sums[0][None], sums[1][None], sums[2].T[None])


def solution(mesh):
    return jax.shard_map(
        local,
        mesh=mesh,
        in_specs=(
            P(("dp", "expert"), None),
            P(("dp", "expert"), None),
            P(("dp", "expert"), None),
            P(("dp", "expert"), None),
            P("expert", None, "tp"),
            P("expert", None, "tp"),
            P("expert", "tp", None),
        ),
        out_specs=(
            P(("dp", "expert"), None),
            P(("dp", "expert"), None),
            P("expert", "dp", "tp"),
            P("expert", "dp", "tp"),
            P("expert", "tp", "dp"),
        ),
        check_vma=False,
    )
```

```python
import jax
import jax.numpy as jnp
from jax import lax
from jax.sharding import PartitionSpec as P

CAP = 6
ROWS = 8
SIDE = 4
STEPS = (2, 1, 3)
F32 = jnp.float32
BF16 = jnp.bfloat16
SWAP = [(0, 1), (1, 0)]


def dot(a, b, ca, cb):
    return lax.dot_general(a, b, (((ca,), (cb,)), ((), ())), preferred_element_type=F32)


def iota(shape, axis):
    return lax.broadcasted_iota(jnp.int32, shape, axis)


def along(axis, step):
    pairs = []
    for y in range(SIDE):
        for x in range(SIDE):
            to = (y, (x + step) % SIDE) if axis == "x" else ((y + step) % SIDE, x)
            pairs.append((y * SIDE + x, to[0] * SIDE + to[1]))
    return pairs


def exchange(stacked, dim, axis, position):
    def piece(step):
        place = (position + step) & (SIDE - 1)
        return lax.dynamic_index_in_dim(stacked, place, dim, keepdims=False)

    got = [lax.ppermute(piece(step), "dp", along(axis, step)) for step in STEPS]
    total = piece(0).astype(F32)
    for other in got:
        total = total + other.astype(F32)
    return total.astype(BF16)


def replica_sum(first_part, second_part):
    place = lax.axis_index("dp").astype(jnp.uint32)
    at_y, at_x = (place // SIDE).astype(jnp.int32), (place & (SIDE - 1)).astype(jnp.int32)
    share = first_part.shape[0] // (SIDE * SIDE)
    first_grid = first_part.reshape(SIDE, SIDE, share, first_part.shape[1])
    second_grid = second_part.reshape(SIDE, SIDE, share, second_part.shape[1])
    first_row = exchange(first_grid, 1, "x", at_x)
    second_row = exchange(second_grid, 0, "y", at_y)
    return exchange(first_row, 0, "y", at_y), exchange(second_row, 0, "x", at_x)


def local(tokens, grad_out, expert_ids, route_probs, w_gate, w_up, w_down):
    toks, width = tokens.shape
    top = expert_ids.shape[1]
    groups = lax.axis_size("expert")
    half = width // 2
    hidden_units = w_gate.shape[2]
    first = lax.axis_index("tp") == 0
    wg, wu, wd = w_gate[0], w_up[0], w_down[0]
    n = toks * top
    slots = groups * ROWS

    flat = expert_ids.reshape(n)
    chosen = (flat[:, None] == iota((n, groups), 1)).astype(BF16)
    lower = (iota((n, n), 1) < iota((n, n), 0)).astype(BF16)
    rank = jnp.sum(dot(lower, chosen, 1, 0) * chosen.astype(F32), axis=1).astype(jnp.int32)
    late = (rank >= 3).astype(jnp.int32)
    placed = (flat * ROWS + rank)[:, None] == iota((n, slots), 1)
    placed_tail = (flat * ROWS + CAP + late)[:, None] == iota((n, slots), 1)
    third = (rank - 3 * late)[:, None]

    def by_token(mask):
        return jnp.any(mask.reshape(toks, top, slots), axis=1).astype(BF16)

    head_map = by_token(placed)
    tail_maps = [by_token(placed_tail & (third == j)) for j in range(3)]

    x_half = jnp.where(first, tokens[:, :half], tokens[:, half:])
    dy_half = jnp.where(first, grad_out[:, :half], grad_out[:, half:])
    both = jnp.concatenate([x_half, dy_half], axis=1)
    quarter = both.shape[1] // 4
    last = both[:, 3 * quarter :]
    pieces = []
    for j in range(3):
        source = jnp.concatenate([both[:, j * quarter : (j + 1) * quarter], last], axis=0)
        lhs = jnp.concatenate([head_map, tail_maps[j]], axis=0)
        pieces.append(dot(lhs, source, 0, 0).astype(BF16))
    spread = jnp.broadcast_to(route_probs.reshape(n, 1), (n, 128))
    pieces.append(dot(placed.astype(BF16), spread, 0, 0).astype(BF16))
    sent = jnp.concatenate(pieces, axis=1).reshape(groups, ROWS, 3 * quarter + 128)
    recv = lax.all_to_all(sent, "expert", split_axis=0, concat_axis=0, tiled=True)
    recv = recv.reshape(slots, 3 * quarter + 128)
    other = lax.ppermute(recv, "tp", SWAP)
    weight = recv[:, 3 * quarter : 3 * quarter + 1].astype(F32)

    to_i, from_i = iota((slots, slots), 0), iota((slots, slots), 1)
    slot_i, row_i = to_i % ROWS, from_i % ROWS
    same = to_i // ROWS == from_i // ROWS

    def tail_of(rows, size):
        total = 0.0
        for j in range(3):
            here = (slot_i == j) & (row_i == CAP) | (slot_i == 3 + j) & (row_i == CAP + 1)
            total += dot((same & here).astype(BF16), rows[:, j * size : (j + 1) * size], 1, 0)
        return total.astype(BF16)

    mine_tail, other_tail = tail_of(recv, quarter), tail_of(other, quarter)
    low, high = jnp.where(first, recv, other), jnp.where(first, other, recv)
    low_tail = jnp.where(first, mine_tail, other_tail)
    high_tail = jnp.where(first, other_tail, mine_tail)
    x = jnp.concatenate([low[:, :half], high[:, :half]], axis=1)
    dy = jnp.concatenate(
        [low[:, half : 3 * quarter], low_tail, high[:, half : 3 * quarter], high_tail], axis=1
    )

    gate = dot(x, wg, 1, 0)
    up = dot(x, wu, 1, 0)
    silu_gate = jax.nn.silu(gate)
    hidden = (silu_gate * up).astype(BF16)
    back = dot(dy, wd, 1, 1)
    prob_part = jnp.sum(hidden.astype(F32) * back, axis=1, keepdims=True).astype(BF16)
    d_hidden = weight * back
    sigma = jax.nn.sigmoid(gate)
    d_gate = (d_hidden * up * sigma * (1.0 + gate * (1.0 - sigma))).astype(BF16)
    d_up = (d_hidden * silu_gate).astype(BF16)
    row_part = dot(d_gate, wg, 1, 1) + dot(d_up, wu, 1, 1)

    mine = jnp.where(first, row_part[:, :half], row_part[:, half:])
    yours = jnp.where(first, row_part[:, half:], row_part[:, :half]).astype(BF16)
    swapped = lax.ppermute(
        jnp.concatenate([yours, jnp.broadcast_to(prob_part, (slots, 128))], axis=1), "tp", SWAP
    )
    d_row = (mine + swapped[:, :half].astype(F32)).astype(BF16)
    prob = (prob_part.astype(F32) + swapped[:, half:].astype(F32)).astype(BF16)
    size = half // 4
    is_slot = iota((slots, 1), 0) % ROWS < CAP
    tail = d_row[:, 3 * size :]
    pieces = []
    for j in range(3):
        here = (row_i == j) & (slot_i == CAP) | (row_i == 3 + j) & (slot_i == CAP + 1)
        moved = dot((same & here).astype(BF16), tail, 1, 0).astype(BF16)
        pieces.append(jnp.where(is_slot, d_row[:, j * size : (j + 1) * size], moved))
    back_sent = jnp.concatenate(pieces + [prob], axis=1).reshape(groups, ROWS, 3 * size + 128)

    back_sent, hidden, d_gate, d_up = lax.optimization_barrier((back_sent, hidden, d_gate, d_up))
    back_recv = lax.all_to_all(back_sent, "expert", split_axis=0, concat_axis=0, tiled=True)
    back_recv = back_recv.reshape(slots, 3 * size + 128)

    scaled = (weight * dy.astype(F32)).astype(BF16)
    cut = 2 * hidden_units // 3
    sum_a, sum_b = replica_sum(
        dot(x, jnp.concatenate([d_gate, d_up[:, :cut]], axis=1), 0, 0).astype(BF16),
        jnp.concatenate(
            [dot(x, d_up[:, cut:], 0, 0).astype(BF16), dot(scaled, hidden, 0, 0).astype(BF16)],
            axis=1,
        ),
    )
    grad_gate = sum_a[:, :hidden_units]
    grad_up = jnp.concatenate([sum_a[:, hidden_units:], sum_b[:, : hidden_units - cut]], axis=1)
    grad_down = sum_b[:, hidden_units - cut :].T

    summed = dot(head_map, back_recv[:, : 3 * size], 1, 0)
    summed_tail = 0.0
    for j in range(3):
        summed_tail += dot(tail_maps[j], back_recv[:, j * size : (j + 1) * size], 1, 0)
    summed = jnp.concatenate([summed, summed_tail], axis=1).astype(BF16)
    summed_other = lax.ppermute(summed, "tp", SWAP)
    d_tokens = jnp.where(
        first,
        jnp.concatenate([summed, summed_other], axis=1),
        jnp.concatenate([summed_other, summed], axis=1),
    )
    d_probs = dot(placed.astype(BF16), back_recv[:, 3 * size :], 1, 0)[:, 0]
    d_probs = d_probs.reshape(toks, top).astype(BF16)
    return (d_tokens, d_probs, grad_gate[None], grad_up[None], grad_down[None])


def solution(mesh):
    return jax.shard_map(
        local,
        mesh=mesh,
        in_specs=(
            P(("dp", "expert"), None),
            P(("dp", "expert"), None),
            P(("dp", "expert"), None),
            P(("dp", "expert"), None),
            P("expert", None, "tp"),
            P("expert", None, "tp"),
            P("expert", "tp", None),
        ),
        out_specs=(
            P(("dp", "expert"), None),
            P(("dp", "expert"), None),
            P("expert", "dp", "tp"),
            P("expert", "dp", "tp"),
            P("expert", "tp", "dp"),
        ),
        check_vma=False,
    )
```

```python
import jax
import jax.numpy as jnp
from jax import lax
from jax.experimental import pallas as pl
from jax.experimental.pallas import tpu as pltpu
from jax.sharding import PartitionSpec as P

CAP = 6
ROWS = 8
SIDE = 4
STEPS = (2, 1, 3)
F32 = jnp.float32
BF16 = jnp.bfloat16
SWAP = [(0, 1), (1, 0)]


def dot(a, b, ca, cb):
    return lax.dot_general(a, b, (((ca,), (cb,)), ((), ())), preferred_element_type=F32)


def iota(shape, axis):
    return lax.broadcasted_iota(jnp.int32, shape, axis)


def along(axis, step):
    pairs = []
    for y in range(SIDE):
        for x in range(SIDE):
            to = (y, (x + step) % SIDE) if axis == "x" else ((y + step) % SIDE, x)
            pairs.append((y * SIDE + x, to[0] * SIDE + to[1]))
    return pairs


def terms_kernel(place, x_ref, dy_ref, weight_ref, d_ref, hidden_ref, *outs):
    a_refs, b_refs = outs[:SIDE], outs[SIDE:]
    split = d_ref.shape[1]
    share = x_ref.shape[1] // (SIDE * SIDE)
    part = share // 2
    weight = weight_ref[...]
    for j in range(SIDE):
        for k in range(SIDE):
            at = ((place[0] + j) & (SIDE - 1)) * SIDE + ((place[1] + k) & (SIDE - 1))
            cols = pl.ds(pl.multiple_of(at * share, share), share)
            scaled = (weight * dy_ref[:, cols].astype(F32)).astype(BF16)
            inner = dot(x_ref[:, cols], d_ref[...], 0, 0).astype(BF16)
            outer = dot(scaled, hidden_ref[...], 0, 0).astype(BF16)
            a_refs[k][j, :, :split] = inner[:part]
            a_refs[k][j, :, split:] = outer[:part]
            b_refs[j][k, :, :split] = inner[part:]
            b_refs[j][k, :, split:] = outer[part:]


def add_up(own, others):
    total = own.astype(F32)
    for other in others:
        total = total + other.astype(F32)
    return total.astype(BF16)


def exchange(pieces, axis):
    got = [lax.ppermute(pieces[step], "dp", along(axis, step)) for step in STEPS]
    return pieces[0], got


def replica_sum(x, dy, weight, d_both, hidden):
    place = lax.axis_index("dp")
    at = jnp.stack([place >> 2, place & (SIDE - 1)]).astype(jnp.int32)
    width, columns = x.shape[1], d_both.shape[1] + hidden.shape[1]
    share = width // (SIDE * SIDE)
    out = jax.ShapeDtypeStruct((SIDE, share // 2, columns), BF16)
    vmem = pl.BlockSpec(memory_space=pltpu.VMEM)
    pieces = pl.pallas_call(
        terms_kernel,
        out_shape=[out] * (2 * SIDE),
        in_specs=[pl.BlockSpec(memory_space=pltpu.SMEM)] + [vmem] * 5,
        out_specs=[vmem] * (2 * SIDE),
        cost_estimate=pl.CostEstimate(
            flops=2 * x.shape[0] * width * columns,
            bytes_accessed=2 * width * columns + 4 * x.size,
            transcendentals=0,
        ),
        name="terms",
    )(at, x, dy, jnp.broadcast_to(weight, (weight.shape[0], share)), d_both, hidden)
    sums = []
    first = [exchange(pieces[:SIDE], "x"), exchange(pieces[SIDE:], "y")]
    for (own, got), axis in zip(first, ("y", "x")):
        rows = [add_up(own[i], [piece[i] for piece in got]) for i in range(SIDE)]
        sums.append(add_up(*exchange(rows, axis)))
    return jnp.concatenate(sums, axis=0)


def local(tokens, grad_out, expert_ids, route_probs, w_gate, w_up, w_down):
    toks, width = tokens.shape
    top = expert_ids.shape[1]
    groups = lax.axis_size("expert")
    half = width // 2
    hidden_units = w_gate.shape[2]
    first = lax.axis_index("tp") == 0
    wg, wu, wd = w_gate[0], w_up[0], w_down[0]
    n = toks * top
    slots = groups * ROWS

    flat = expert_ids.reshape(n)
    chosen = (flat[:, None] == iota((n, groups), 1)).astype(BF16)
    lower = (iota((n, n), 1) < iota((n, n), 0)).astype(BF16)
    rank = jnp.sum(dot(lower, chosen, 1, 0) * chosen.astype(F32), axis=1).astype(jnp.int32)
    late = (rank >= 3).astype(jnp.int32)
    placed = (flat * ROWS + rank)[:, None] == iota((n, slots), 1)
    placed_tail = (flat * ROWS + CAP + late)[:, None] == iota((n, slots), 1)
    third = (rank - 3 * late)[:, None]

    def by_token(mask):
        return jnp.any(mask.reshape(toks, top, slots), axis=1).astype(BF16)

    head_map = by_token(placed)
    tail_maps = [by_token(placed_tail & (third == j)) for j in range(3)]

    x_half = jnp.where(first, tokens[:, :half], tokens[:, half:])
    dy_half = jnp.where(first, grad_out[:, :half], grad_out[:, half:])
    both = jnp.concatenate([x_half, dy_half], axis=1)
    quarter = both.shape[1] // 4
    last = both[:, 3 * quarter :]
    pieces = []
    for j in range(3):
        source = jnp.concatenate([both[:, j * quarter : (j + 1) * quarter], last], axis=0)
        lhs = jnp.concatenate([head_map, tail_maps[j]], axis=0)
        pieces.append(dot(lhs, source, 0, 0).astype(BF16))
    spread = jnp.broadcast_to(route_probs.reshape(n, 1), (n, 128))
    pieces.append(dot(placed.astype(BF16), spread, 0, 0).astype(BF16))
    sent = jnp.concatenate(pieces, axis=1).reshape(groups, ROWS, 3 * quarter + 128)
    recv = lax.all_to_all(sent, "expert", split_axis=0, concat_axis=0, tiled=True)
    recv = recv.reshape(slots, 3 * quarter + 128)
    other = lax.ppermute(recv, "tp", SWAP)
    weight = recv[:, 3 * quarter : 3 * quarter + 1].astype(F32)

    to_i, from_i = iota((slots, slots), 0), iota((slots, slots), 1)
    slot_i, row_i = to_i % ROWS, from_i % ROWS
    same = to_i // ROWS == from_i // ROWS

    def tail_of(rows, size):
        total = 0.0
        for j in range(3):
            here = (slot_i == j) & (row_i == CAP) | (slot_i == 3 + j) & (row_i == CAP + 1)
            total += dot((same & here).astype(BF16), rows[:, j * size : (j + 1) * size], 1, 0)
        return total.astype(BF16)

    mine_tail, other_tail = tail_of(recv, quarter), tail_of(other, quarter)
    low, high = jnp.where(first, recv, other), jnp.where(first, other, recv)
    low_tail = jnp.where(first, mine_tail, other_tail)
    high_tail = jnp.where(first, other_tail, mine_tail)
    x = jnp.concatenate([low[:, :half], high[:, :half]], axis=1)
    dy = jnp.concatenate(
        [low[:, half : 3 * quarter], low_tail, high[:, half : 3 * quarter], high_tail], axis=1
    )

    gate = dot(x, wg, 1, 0)
    up = dot(x, wu, 1, 0)
    silu_gate = jax.nn.silu(gate)
    hidden = (silu_gate * up).astype(BF16)
    back = dot(dy, wd, 1, 1)
    prob_part = jnp.sum(hidden.astype(F32) * back, axis=1, keepdims=True).astype(BF16)
    d_hidden = weight * back
    sigma = jax.nn.sigmoid(gate)
    d_gate = (d_hidden * up * sigma * (1.0 + gate * (1.0 - sigma))).astype(BF16)
    d_up = (d_hidden * silu_gate).astype(BF16)
    row_part = dot(d_gate, wg, 1, 1) + dot(d_up, wu, 1, 1)

    mine = jnp.where(first, row_part[:, :half], row_part[:, half:])
    yours = jnp.where(first, row_part[:, half:], row_part[:, :half]).astype(BF16)
    swapped = lax.ppermute(
        jnp.concatenate([yours, jnp.broadcast_to(prob_part, (slots, 128))], axis=1), "tp", SWAP
    )
    d_row = (mine + swapped[:, :half].astype(F32)).astype(BF16)
    prob = (prob_part.astype(F32) + swapped[:, half:].astype(F32)).astype(BF16)
    size = half // 4
    is_slot = iota((slots, 1), 0) % ROWS < CAP
    tail = d_row[:, 3 * size :]
    pieces = []
    for j in range(3):
        here = (row_i == j) & (slot_i == CAP) | (row_i == 3 + j) & (slot_i == CAP + 1)
        moved = dot((same & here).astype(BF16), tail, 1, 0).astype(BF16)
        pieces.append(jnp.where(is_slot, d_row[:, j * size : (j + 1) * size], moved))
    back_sent = jnp.concatenate(pieces + [prob], axis=1).reshape(groups, ROWS, 3 * size + 128)

    back_sent, hidden, d_gate, d_up = lax.optimization_barrier((back_sent, hidden, d_gate, d_up))
    back_recv = lax.all_to_all(back_sent, "expert", split_axis=0, concat_axis=0, tiled=True)
    back_recv = back_recv.reshape(slots, 3 * size + 128)

    d_both = jnp.concatenate([d_gate, d_up], axis=1)
    grads = replica_sum(x, dy, weight, d_both, hidden)
    grad_gate, grad_up = grads[:, :hidden_units], grads[:, hidden_units : 2 * hidden_units]
    grad_down = grads[:, 2 * hidden_units :].T

    summed = dot(head_map, back_recv[:, : 3 * size], 1, 0)
    summed_tail = 0.0
    for j in range(3):
        summed_tail += dot(tail_maps[j], back_recv[:, j * size : (j + 1) * size], 1, 0)
    summed = jnp.concatenate([summed, summed_tail], axis=1).astype(BF16)
    summed_other = lax.ppermute(summed, "tp", SWAP)
    d_tokens = jnp.where(
        first,
        jnp.concatenate([summed, summed_other], axis=1),
        jnp.concatenate([summed_other, summed], axis=1),
    )
    d_probs = dot(placed.astype(BF16), back_recv[:, 3 * size :], 1, 0)[:, 0]
    d_probs = d_probs.reshape(toks, top).astype(BF16)
    return (d_tokens, d_probs, grad_gate[None], grad_up[None], grad_down[None])


def solution(mesh):
    return jax.shard_map(
        local,
        mesh=mesh,
        in_specs=(
            P(("dp", "expert"), None),
            P(("dp", "expert"), None),
            P(("dp", "expert"), None),
            P(("dp", "expert"), None),
            P("expert", None, "tp"),
            P("expert", None, "tp"),
            P("expert", "tp", None),
        ),
        out_specs=(
            P(("dp", "expert"), None),
            P(("dp", "expert"), None),
            P("expert", "dp", "tp"),
            P("expert", "dp", "tp"),
            P("expert", "tp", "dp"),
        ),
        check_vma=False,
    )
```

```python
import jax
import jax.numpy as jnp
from jax import lax
from jax.experimental import pallas as pl
from jax.experimental.pallas import tpu as pltpu
from jax.sharding import PartitionSpec as P


CAP = 6
ROWS = 8
SIDE = 4
STEPS = (2, 1, 3)
F32 = jnp.float32
BF16 = jnp.bfloat16
SWAP = [(0, 1), (1, 0)]


def dot(a, b, ca, cb):
    return lax.dot_general(a, b, (((ca,), (cb,)), ((), ())), preferred_element_type=F32)


def iota(shape, axis):
    return lax.broadcasted_iota(jnp.int32, shape, axis)


def along(axis, step):
    pairs = []
    for y in range(SIDE):
        for x in range(SIDE):
            to = (y, (x + step) % SIDE) if axis == "x" else ((y + step) % SIDE, x)
            pairs.append((y * SIDE + x, to[0] * SIDE + to[1]))
    return pairs


def terms_kernel(place, x_ref, dy_ref, weight_ref, gate_ref, up_ref, hidden_ref, *outs):
    a_refs, b_refs = outs[:SIDE], outs[SIDE:]
    units = hidden_ref.shape[1]
    share = x_ref.shape[1] // (SIDE * SIDE)
    part = share // 2
    weight = weight_ref[...]
    for j in range(SIDE):
        for k in range(SIDE):
            at = ((place[0] + j) & (SIDE - 1)) * SIDE + ((place[1] + k) & (SIDE - 1))
            cols = pl.ds(pl.multiple_of(at * share, share), share)
            scaled = (weight * dy_ref[:, cols].astype(F32)).astype(BF16)
            xs = x_ref[:, cols]
            terms = (
                dot(xs, gate_ref[...], 0, 0),
                dot(xs, up_ref[...], 0, 0),
                dot(scaled, hidden_ref[...], 0, 0),
            )
            for i, term in enumerate(terms):
                rounded = term.astype(BF16)
                a_refs[k][j, :, i * units : (i + 1) * units] = rounded[:part]
                b_refs[j][k, :, i * units : (i + 1) * units] = rounded[part:]


def add_up(own, others):
    total = own.astype(F32)
    for other in others:
        total = total + other.astype(F32)
    return total.astype(BF16)


def exchange(pieces, axis):
    got = [lax.ppermute(pieces[step], "dp", along(axis, step)) for step in STEPS]
    return pieces[0], got


def replica_sum(x, dy, weight, d_gate, d_up, hidden):
    place = lax.axis_index("dp")
    at = jnp.stack([place >> 2, place & (SIDE - 1)]).astype(jnp.int32)
    width, columns = x.shape[1], 3 * hidden.shape[1]
    share = width // (SIDE * SIDE)
    out = jax.ShapeDtypeStruct((SIDE, share // 2, columns), BF16)
    vmem = pl.BlockSpec(memory_space=pltpu.VMEM)
    pieces = pl.pallas_call(
        terms_kernel,
        out_shape=[out] * (2 * SIDE),
        in_specs=[pl.BlockSpec(memory_space=pltpu.SMEM)] + [vmem] * 6,
        out_specs=[vmem] * (2 * SIDE),
        cost_estimate=pl.CostEstimate(
            flops=2 * x.shape[0] * width * columns,
            bytes_accessed=2 * width * columns + 4 * x.size,
            transcendentals=0,
        ),
        name="terms",
    )(at, x, dy, weight, d_gate, d_up, hidden)
    sums = []
    first = [exchange(pieces[:SIDE], "x"), exchange(pieces[SIDE:], "y")]
    for (own, got), axis in zip(first, ("y", "x")):
        rows = [add_up(own[i], [piece[i] for piece in got]) for i in range(SIDE)]
        sums.append(add_up(*exchange(rows, axis)))
    return jnp.concatenate(sums, axis=0)


def gather_half(block, groups, first):
    pair = ("expert", "tp")
    above = [(2 * z + 1, 2 * ((z - 1) % groups) + 1) for z in range(groups)]
    hop = lax.ppermute(block, pair, above)
    held = jnp.where(first, block, hop)[None]
    step = groups // 4
    while step:
        both_ways = [
            (2 * z + core, 2 * ((z + (-step if core else step)) % groups) + core)
            for z in range(groups)
            for core in range(2)
        ]
        held = jnp.concatenate([held, lax.ppermute(held, pair, both_ways)], axis=0)
        step //= 2
    return held


def local(tokens, grad_out, expert_ids, route_probs, w_gate, w_up, w_down):
    toks, width = tokens.shape
    top = expert_ids.shape[1]
    groups = lax.axis_size("expert")
    half = width // 2
    hidden_units = w_gate.shape[2]
    first = lax.axis_index("tp") == 0
    wg, wu, wd = w_gate[0], w_up[0], w_down[0]
    n = toks * top
    slots = groups * ROWS

    flat = expert_ids.reshape(n)
    chosen = (flat[:, None] == iota((n, groups), 1)).astype(BF16)
    lower = (iota((n, n), 1) < iota((n, n), 0)).astype(BF16)
    rank = jnp.sum(dot(lower, chosen, 1, 0) * chosen.astype(F32), axis=1).astype(jnp.int32)
    late = (rank >= 3).astype(jnp.int32)
    placed = (flat * ROWS + rank)[:, None] == iota((n, slots), 1)
    placed_tail = (flat * ROWS + CAP + late)[:, None] == iota((n, slots), 1)
    third = (rank - 3 * late)[:, None]

    def by_token(mask):
        return jnp.any(mask.reshape(toks, top, slots), axis=1).astype(BF16)

    head_map = by_token(placed)
    tail_maps = [by_token(placed_tail & (third == j)) for j in range(3)]

    size = half // 4
    x_half = jnp.where(first, tokens[:, :half], tokens[:, half:])
    pieces = []
    for j in range(3):
        source = [x_half[:, j * size : (j + 1) * size], x_half[:, 3 * size :]]
        lhs = jnp.concatenate([head_map, tail_maps[j]], axis=0)
        pieces.append(dot(lhs, jnp.concatenate(source, axis=0), 0, 0).astype(BF16))
    sent = jnp.concatenate(pieces, axis=1).reshape(groups, ROWS, 3 * size)
    side = jnp.pad(
        jnp.concatenate([expert_ids.astype(BF16), route_probs], axis=1),
        ((0, 0), (0, 128 - 2 * top)),
    )
    own = jnp.concatenate([grad_out, side], axis=1)
    sent, own = lax.optimization_barrier((sent, own))
    recv = lax.all_to_all(sent, "expert", split_axis=0, concat_axis=0, tiled=True)
    recv = recv.reshape(slots, 3 * size)
    other = lax.ppermute(recv, "tp", SWAP)

    seen = gather_half(own, groups, first)
    blocks = seen.shape[0]
    rows = blocks * toks
    seen = seen.reshape(rows, width + 128)
    me = lax.axis_index("expert")
    index = iota((rows, 1), 0) // toks
    away, bits = jnp.zeros((rows, 1), jnp.int32), blocks.bit_length() - 1
    for i in range(bits):
        away = away + ((index >> i) & 1) * (1 << (bits - 1 - i))
    block = (jnp.where(first, me - away, me + 1 + away) + groups) % groups
    named = seen[:, width : width + top].astype(jnp.int32) == me
    hit = jnp.any(named, axis=1, keepdims=True)
    p_row = jnp.sum(
        jnp.where(named, seen[:, width + top : width + 2 * top].astype(F32), 0.0),
        axis=1,
        keepdims=True,
    ).astype(BF16)
    one, two = iota((rows, rows), 0), iota((rows, rows), 1)
    before = ((two < one) & (two // toks == one // toks)).astype(BF16)
    ahead = dot(before, jnp.broadcast_to(hit.astype(BF16), (rows, 128)), 1, 0)[:, :1]
    place = jnp.where(hit, block * ROWS + ahead.astype(jnp.int32), -1)
    pick = (place == iota((rows, slots), 1)).astype(BF16)
    source = jnp.concatenate([seen[:, :width], jnp.broadcast_to(p_row, (rows, 128))], axis=1)
    mine = dot(pick, source, 0, 0).astype(BF16)
    both = mine + lax.ppermute(mine, "tp", SWAP)
    dy, weights = both[:, :width], both[:, width:].astype(F32)
    weight = weights[:, :1]

    to_i, from_i = iota((slots, slots), 0), iota((slots, slots), 1)
    slot_i, row_i = to_i % ROWS, from_i % ROWS
    same = to_i // ROWS == from_i // ROWS

    def tail_of(rows, size):
        total = 0.0
        for j in range(3):
            here = (slot_i == j) & (row_i == CAP) | (slot_i == 3 + j) & (row_i == CAP + 1)
            total += dot((same & here).astype(BF16), rows[:, j * size : (j + 1) * size], 1, 0)
        return total.astype(BF16)

    mine_tail, other_tail = tail_of(recv, size), tail_of(other, size)
    mine_all = jnp.concatenate([recv, mine_tail], axis=1)
    other_all = jnp.concatenate([other, other_tail], axis=1)
    x = jnp.concatenate(
        [jnp.where(first, mine_all, other_all), jnp.where(first, other_all, mine_all)], axis=1
    )

    gate = dot(x, wg, 1, 0)
    up = dot(x, wu, 1, 0)
    silu_gate = jax.nn.silu(gate)
    hidden = (silu_gate * up).astype(BF16)
    back = dot(dy, wd, 1, 1)
    prob_part = jnp.sum(hidden.astype(F32) * back, axis=1, keepdims=True).astype(BF16)
    d_hidden = weight * back
    sigma = jax.nn.sigmoid(gate)
    d_gate = (d_hidden * up * sigma * (1.0 + gate * (1.0 - sigma))).astype(BF16)
    d_up = (d_hidden * silu_gate).astype(BF16)
    row_part = dot(d_gate, wg, 1, 1) + dot(d_up, wu, 1, 1)

    mine = jnp.where(first, row_part[:, :half], row_part[:, half:])
    yours = jnp.where(first, row_part[:, half:], row_part[:, :half]).astype(BF16)
    swapped = lax.ppermute(
        jnp.concatenate([yours, jnp.broadcast_to(prob_part, (slots, 128))], axis=1), "tp", SWAP
    )
    d_row = (mine + swapped[:, :half].astype(F32)).astype(BF16)
    prob = (prob_part.astype(F32) + swapped[:, half:].astype(F32)).astype(BF16)
    is_slot = iota((slots, 1), 0) % ROWS < CAP
    tail = d_row[:, 3 * size :]
    pieces = []
    for j in range(3):
        here = (row_i == j) & (slot_i == CAP) | (row_i == 3 + j) & (slot_i == CAP + 1)
        moved = dot((same & here).astype(BF16), tail, 1, 0).astype(BF16)
        pieces.append(jnp.where(is_slot, d_row[:, j * size : (j + 1) * size], moved))
    back_sent = jnp.concatenate(pieces + [prob], axis=1).reshape(groups, ROWS, 3 * size + 128)

    back_sent, hidden, d_gate, d_up = lax.optimization_barrier((back_sent, hidden, d_gate, d_up))
    back_recv = lax.all_to_all(back_sent, "expert", split_axis=0, concat_axis=0, tiled=True)
    back_recv = back_recv.reshape(slots, 3 * size + 128)

    grads = replica_sum(x, dy, weights, d_gate, d_up, hidden)
    grad_gate, grad_up = grads[:, :hidden_units], grads[:, hidden_units : 2 * hidden_units]
    grad_down = grads[:, 2 * hidden_units :].T

    summed = dot(head_map, back_recv[:, : 3 * size], 1, 0)
    summed_tail = 0.0
    for j in range(3):
        summed_tail += dot(tail_maps[j], back_recv[:, j * size : (j + 1) * size], 1, 0)
    summed = jnp.concatenate([summed, summed_tail], axis=1).astype(BF16)
    summed_other = lax.ppermute(summed, "tp", SWAP)
    d_tokens = jnp.where(
        first,
        jnp.concatenate([summed, summed_other], axis=1),
        jnp.concatenate([summed_other, summed], axis=1),
    )
    d_probs = dot(placed.astype(BF16), back_recv[:, 3 * size :], 1, 0)[:, 0]
    d_probs = d_probs.reshape(toks, top).astype(BF16)
    return (d_tokens, d_probs, grad_gate[None], grad_up[None], grad_down[None])


def solution(mesh):
    return jax.shard_map(
        local,
        mesh=mesh,
        in_specs=(
            P(("dp", "expert"), None),
            P(("dp", "expert"), None),
            P(("dp", "expert"), None),
            P(("dp", "expert"), None),
            P("expert", None, "tp"),
            P("expert", None, "tp"),
            P("expert", "tp", None),
        ),
        out_specs=(
            P(("dp", "expert"), None),
            P(("dp", "expert"), None),
            P("expert", "dp", "tp"),
            P("expert", "dp", "tp"),
            P("expert", "tp", "dp"),
        ),
        check_vma=False,
    )
```

```python
import jax
import jax.numpy as jnp
from jax import lax
from jax.experimental import pallas as pl
from jax.experimental.pallas import tpu as pltpu
from jax.sharding import PartitionSpec as P

CAP = 6
ROWS = 8
SIDE = 4
STEPS = (2, 1, 3)
F32 = jnp.float32
BF16 = jnp.bfloat16
SWAP = [(0, 1), (1, 0)]


def dot(a, b, ca, cb):
    return lax.dot_general(a, b, (((ca,), (cb,)), ((), ())), preferred_element_type=F32)


def iota(shape, axis):
    return lax.broadcasted_iota(jnp.int32, shape, axis)


def along(step, across):
    pairs = []
    for y in range(SIDE):
        for x in range(SIDE):
            for core in range(2):
                if core == across:
                    to = y * SIDE + (x + step) % SIDE
                else:
                    to = (y + step) % SIDE * SIDE + x
                pairs.append((2 * (y * SIDE + x) + core, 2 * to + core))
    return pairs


def terms_kernel(at, x_ref, dy_ref, recv_ref, gate_ref, up_ref, hidden_ref, *outs):
    units = hidden_ref.shape[1]
    share = x_ref.shape[1] // (SIDE * SIDE)
    weight = recv_ref[:, recv_ref.shape[1] - share :].astype(F32)
    for i in range(SIDE):
        for l in range(SIDE):
            y = (at[0] + jnp.where(at[2] == 0, l, i)) & (SIDE - 1)
            x = (at[1] + jnp.where(at[2] == 0, i, l)) & (SIDE - 1)
            cols = pl.ds(pl.multiple_of((y * SIDE + x) * share, share), share)
            scaled = (weight * dy_ref[:, cols].astype(F32)).astype(BF16)
            xs = x_ref[:, cols]
            outs[i][l, :, :units] = dot(xs, gate_ref[...], 0, 0).astype(BF16)
            outs[i][l, :, units : 2 * units] = dot(xs, up_ref[...], 0, 0).astype(BF16)
            outs[i][l, :, 2 * units :] = dot(scaled, hidden_ref[...], 0, 0).astype(BF16)


def exchange(pieces, across):
    got = [lax.ppermute(pieces[step], ("dp", "tp"), along(step, across)) for step in STEPS]
    return [pieces[0]] + got


def add_up(arrays):
    return sum(array.astype(F32) for array in arrays).astype(BF16)


def replica_sum(x, dy, recv, d_gate, d_up, hidden):
    place = lax.axis_index("dp")
    at = jnp.stack([place >> 2, place & (SIDE - 1), lax.axis_index("tp")]).astype(jnp.int32)
    width, columns = x.shape[1], 3 * hidden.shape[1]
    share = width // (SIDE * SIDE)
    out = jax.ShapeDtypeStruct((SIDE, share, columns), BF16)
    vmem = pl.BlockSpec(memory_space=pltpu.VMEM)
    pieces = pl.pallas_call(
        terms_kernel,
        out_shape=[out] * SIDE,
        in_specs=[pl.BlockSpec(memory_space=pltpu.SMEM)] + [vmem] * 6,
        out_specs=[vmem] * SIDE,
        cost_estimate=pl.CostEstimate(
            flops=2 * x.shape[0] * width * columns,
            bytes_accessed=2 * width * columns + 4 * x.size,
            transcendentals=0,
        ),
        name="terms",
    )(at, x, dy, recv, d_gate, d_up, hidden)
    near = exchange(pieces, 0)
    rows = [add_up([piece[l] for piece in near]) for l in range(SIDE)]
    return add_up(exchange(rows, 1))


def local(tokens, grad_out, expert_ids, route_probs, w_gate, w_up, w_down):
    toks, width = tokens.shape
    top = expert_ids.shape[1]
    groups = lax.axis_size("expert")
    half = width // 2
    hidden_units = w_gate.shape[2]
    first = lax.axis_index("tp") == 0
    wg, wu, wd = w_gate[0], w_up[0], w_down[0]
    n = toks * top
    slots = groups * ROWS

    flat = expert_ids.reshape(n)
    chosen = (flat[:, None] == iota((n, groups), 1)).astype(BF16)
    lower = (iota((n, n), 1) < iota((n, n), 0)).astype(BF16)
    rank = jnp.sum(dot(lower, chosen, 1, 0) * chosen.astype(F32), axis=1).astype(jnp.int32)
    late = (rank >= 3).astype(jnp.int32)
    placed = (flat * ROWS + rank)[:, None] == iota((n, slots), 1)
    placed_tail = (flat * ROWS + CAP + late)[:, None] == iota((n, slots), 1)
    third = (rank - 3 * late)[:, None]

    def by_token(mask):
        return jnp.any(mask.reshape(toks, top, slots), axis=1).astype(BF16)

    head_map = by_token(placed)
    tail_maps = [by_token(placed_tail & (third == j)) for j in range(3)]

    x_half = jnp.where(first, tokens[:, :half], tokens[:, half:])
    dy_half = jnp.where(first, grad_out[:, :half], grad_out[:, half:])
    both = jnp.concatenate([x_half, dy_half], axis=1)
    quarter = both.shape[1] // 4
    last = both[:, 3 * quarter :]
    pieces = []
    for j in range(3):
        source = jnp.concatenate([both[:, j * quarter : (j + 1) * quarter], last], axis=0)
        lhs = jnp.concatenate([head_map, tail_maps[j]], axis=0)
        pieces.append(dot(lhs, source, 0, 0).astype(BF16))
    spread = jnp.broadcast_to(route_probs.reshape(n, 1), (n, 128))
    pieces.append(dot(placed.astype(BF16), spread, 0, 0).astype(BF16))
    sent = jnp.concatenate(pieces, axis=1).reshape(groups, ROWS, 3 * quarter + 128)
    recv = lax.all_to_all(sent, "expert", split_axis=0, concat_axis=0, tiled=True)
    recv = recv.reshape(slots, 3 * quarter + 128)
    other = lax.ppermute(recv, "tp", SWAP)
    weight = recv[:, 3 * quarter : 3 * quarter + 1].astype(F32)

    to_i, from_i = iota((slots, slots), 0), iota((slots, slots), 1)
    slot_i, row_i = to_i % ROWS, from_i % ROWS
    same = to_i // ROWS == from_i // ROWS

    def tail_of(rows, size):
        total = 0.0
        for j in range(3):
            here = (slot_i == j) & (row_i == CAP) | (slot_i == 3 + j) & (row_i == CAP + 1)
            total += dot((same & here).astype(BF16), rows[:, j * size : (j + 1) * size], 1, 0)
        return total.astype(BF16)

    mine_tail, other_tail = tail_of(recv, quarter), tail_of(other, quarter)
    low, high = jnp.where(first, recv, other), jnp.where(first, other, recv)
    low_tail = jnp.where(first, mine_tail, other_tail)
    high_tail = jnp.where(first, other_tail, mine_tail)
    x = jnp.concatenate([low[:, :half], high[:, :half]], axis=1)
    dy = jnp.concatenate(
        [low[:, half : 3 * quarter], low_tail, high[:, half : 3 * quarter], high_tail], axis=1
    )

    gate = dot(x, wg, 1, 0)
    up = dot(x, wu, 1, 0)
    silu_gate = jax.nn.silu(gate)
    hidden = (silu_gate * up).astype(BF16)
    back = dot(dy, wd, 1, 1)
    prob_part = jnp.sum(hidden.astype(F32) * back, axis=1, keepdims=True).astype(BF16)
    d_hidden = weight * back
    sigma = jax.nn.sigmoid(gate)
    d_gate = (d_hidden * up * sigma * (1.0 + gate * (1.0 - sigma))).astype(BF16)
    d_up = (d_hidden * silu_gate).astype(BF16)
    row_part = dot(d_gate, wg, 1, 1) + dot(d_up, wu, 1, 1)

    mine = jnp.where(first, row_part[:, :half], row_part[:, half:])
    yours = jnp.where(first, row_part[:, half:], row_part[:, :half]).astype(BF16)
    swapped = lax.ppermute(
        jnp.concatenate([yours, jnp.broadcast_to(prob_part, (slots, 128))], axis=1), "tp", SWAP
    )
    d_row = (mine + swapped[:, :half].astype(F32)).astype(BF16)
    prob = (prob_part.astype(F32) + swapped[:, half:].astype(F32)).astype(BF16)
    size = half // 4
    is_slot = iota((slots, 1), 0) % ROWS < CAP
    tail = d_row[:, 3 * size :]
    pieces = []
    for j in range(3):
        here = (row_i == j) & (slot_i == CAP) | (row_i == 3 + j) & (slot_i == CAP + 1)
        moved = dot((same & here).astype(BF16), tail, 1, 0).astype(BF16)
        pieces.append(jnp.where(is_slot, d_row[:, j * size : (j + 1) * size], moved))
    back_sent = jnp.concatenate(pieces + [prob], axis=1).reshape(groups, ROWS, 3 * size + 128)

    back_sent, hidden, d_gate, d_up = lax.optimization_barrier((back_sent, hidden, d_gate, d_up))
    back_recv = lax.all_to_all(back_sent, "expert", split_axis=0, concat_axis=0, tiled=True)
    back_recv = back_recv.reshape(slots, 3 * size + 128)

    grads = replica_sum(x, dy, recv, d_gate, d_up, hidden)
    grad_gate, grad_up = grads[:, :hidden_units], grads[:, hidden_units : 2 * hidden_units]
    grad_down = grads[:, 2 * hidden_units :].T

    summed = dot(head_map, back_recv[:, : 3 * size], 1, 0)
    summed_tail = 0.0
    for j in range(3):
        summed_tail += dot(tail_maps[j], back_recv[:, j * size : (j + 1) * size], 1, 0)
    summed = jnp.concatenate([summed, summed_tail], axis=1).astype(BF16)
    summed_other = lax.ppermute(summed, "tp", SWAP)
    d_tokens = jnp.where(
        first,
        jnp.concatenate([summed, summed_other], axis=1),
        jnp.concatenate([summed_other, summed], axis=1),
    )
    d_probs = dot(placed.astype(BF16), back_recv[:, 3 * size :], 1, 0)[:, 0]
    d_probs = d_probs.reshape(toks, top).astype(BF16)
    return (d_tokens, d_probs, grad_gate[None], grad_up[None], grad_down[None])


def solution(mesh):
    return jax.shard_map(
        local,
        mesh=mesh,
        in_specs=(
            P(("dp", "expert"), None),
            P(("dp", "expert"), None),
            P(("dp", "expert"), None),
            P(("dp", "expert"), None),
            P("expert", None, "tp"),
            P("expert", None, "tp"),
            P("expert", "tp", None),
        ),
        out_specs=(
            P(("dp", "expert"), None),
            P(("dp", "expert"), None),
            P("expert", "dp", "tp"),
            P("expert", "dp", "tp"),
            P("expert", "tp", "dp"),
        ),
        check_vma=False,
    )
```

```python
import jax
import jax.numpy as jnp
from jax import lax
from jax.experimental import pallas as pl
from jax.experimental.pallas import tpu as pltpu
from jax.sharding import PartitionSpec as P

CAP = 6
ROWS = 8
SIDE = 4
STEPS = (2, 1, 3)
F32 = jnp.float32
BF16 = jnp.bfloat16
SWAP = [(0, 1), (1, 0)]


def dot(a, b, ca, cb):
    return lax.dot_general(a, b, (((ca,), (cb,)), ((), ())), preferred_element_type=F32)


def iota(shape, axis):
    return lax.broadcasted_iota(jnp.int32, shape, axis)


def along(step, across):
    pairs = []
    for y in range(SIDE):
        for x in range(SIDE):
            for core in range(2):
                if core == across:
                    to = y * SIDE + (x + step) % SIDE
                else:
                    to = (y + step) % SIDE * SIDE + x
                pairs.append((2 * (y * SIDE + x) + core, 2 * to + core))
    return pairs


def terms_kernel(at, low, high, low_tail, high_tail, gate_ref, up_ref, hidden_ref, *outs):
    units = hidden_ref.shape[1]
    share = low_tail.shape[1] // SIDE
    weight = low[:, low.shape[1] - share :].astype(F32)

    def columns(pair, index, upper):
        cols = pl.ds(pl.multiple_of(index * share, share), share)
        return jnp.where(upper, pair[1][:, cols], pair[0][:, cols])

    for i in range(SIDE):
        for l in range(SIDE):
            y = (at[0] + jnp.where(at[2] == 0, l, i)) & (SIDE - 1)
            x = (at[1] + jnp.where(at[2] == 0, i, l)) & (SIDE - 1)
            half_at, upper = (y & 1) * SIDE + x, y >= 2
            xs = columns((low, high), half_at, upper)
            dy = jnp.where(
                (y & 1) == 0,
                columns((low, high), 2 * SIDE + x, upper),
                columns((low_tail, high_tail), x, upper),
            )
            scaled = (weight * dy.astype(F32)).astype(BF16)
            outs[i][l, :, :units] = dot(xs, gate_ref[...], 0, 0).astype(BF16)
            outs[i][l, :, units : 2 * units] = dot(xs, up_ref[...], 0, 0).astype(BF16)
            outs[i][l, :, 2 * units :] = dot(scaled, hidden_ref[...], 0, 0).astype(BF16)


def exchange(pieces, across):
    got = [lax.ppermute(pieces[step], ("dp", "tp"), along(step, across)) for step in STEPS]
    return [pieces[0]] + got


def add_up(arrays):
    return sum(array.astype(F32) for array in arrays).astype(BF16)


def replica_sum(low, high, low_tail, high_tail, d_gate, d_up, hidden):
    place = lax.axis_index("dp")
    at = jnp.stack([place >> 2, place & (SIDE - 1), lax.axis_index("tp")]).astype(jnp.int32)
    share, columns = low_tail.shape[1] // SIDE, 3 * hidden.shape[1]
    width = share * SIDE * SIDE
    out = jax.ShapeDtypeStruct((SIDE, share, columns), BF16)
    vmem = pl.BlockSpec(memory_space=pltpu.VMEM)
    pieces = pl.pallas_call(
        terms_kernel,
        out_shape=[out] * SIDE,
        in_specs=[pl.BlockSpec(memory_space=pltpu.SMEM)] + [vmem] * 7,
        out_specs=[vmem] * SIDE,
        cost_estimate=pl.CostEstimate(
            flops=2 * low.shape[0] * width * columns,
            bytes_accessed=2 * width * columns + 4 * low.size,
            transcendentals=0,
        ),
        name="terms",
    )(at, low, high, low_tail, high_tail, d_gate, d_up, hidden)
    near = exchange(pieces, 0)
    rows = [add_up([piece[l] for piece in near]) for l in range(SIDE)]
    return add_up(exchange(rows, 1))


def local(tokens, grad_out, expert_ids, route_probs, w_gate, w_up, w_down):
    toks, width = tokens.shape
    top = expert_ids.shape[1]
    groups = lax.axis_size("expert")
    half = width // 2
    hidden_units = w_gate.shape[2]
    first = lax.axis_index("tp") == 0
    wg, wu, wd = w_gate[0], w_up[0], w_down[0]
    n = toks * top
    slots = groups * ROWS

    flat = expert_ids.reshape(n)
    chosen = (flat[:, None] == iota((n, groups), 1)).astype(BF16)
    lower = (iota((n, n), 1) < iota((n, n), 0)).astype(BF16)
    rank = jnp.sum(dot(lower, chosen, 1, 0) * chosen.astype(F32), axis=1).astype(jnp.int32)
    late = (rank >= 3).astype(jnp.int32)
    placed = (flat * ROWS + rank)[:, None] == iota((n, slots), 1)
    placed_tail = (flat * ROWS + CAP + late)[:, None] == iota((n, slots), 1)
    third = (rank - 3 * late)[:, None]

    def by_token(mask):
        return jnp.any(mask.reshape(toks, top, slots), axis=1).astype(BF16)

    head_map = by_token(placed)
    tail_maps = [by_token(placed_tail & (third == j)) for j in range(3)]

    x_half = jnp.where(first, tokens[:, :half], tokens[:, half:])
    dy_half = jnp.where(first, grad_out[:, :half], grad_out[:, half:])
    both = jnp.concatenate([x_half, dy_half], axis=1)
    quarter = both.shape[1] // 4
    last = both[:, 3 * quarter :]
    pieces = []
    for j in range(3):
        source = jnp.concatenate([both[:, j * quarter : (j + 1) * quarter], last], axis=0)
        lhs = jnp.concatenate([head_map, tail_maps[j]], axis=0)
        pieces.append(dot(lhs, source, 0, 0).astype(BF16))
    spread = jnp.broadcast_to(route_probs.reshape(n, 1), (n, 128))
    pieces.append(dot(placed.astype(BF16), spread, 0, 0).astype(BF16))
    sent = jnp.concatenate(pieces, axis=1).reshape(groups, ROWS, 3 * quarter + 128)
    recv = lax.all_to_all(sent, "expert", split_axis=0, concat_axis=0, tiled=True)
    recv = recv.reshape(slots, 3 * quarter + 128)
    other = lax.ppermute(recv, "tp", SWAP)
    weight = recv[:, 3 * quarter : 3 * quarter + 1].astype(F32)

    to_i, from_i = iota((slots, slots), 0), iota((slots, slots), 1)
    slot_i, row_i = to_i % ROWS, from_i % ROWS
    same = to_i // ROWS == from_i // ROWS

    def tail_of(rows, size):
        total = 0.0
        for j in range(3):
            here = (slot_i == j) & (row_i == CAP) | (slot_i == 3 + j) & (row_i == CAP + 1)
            total += dot((same & here).astype(BF16), rows[:, j * size : (j + 1) * size], 1, 0)
        return total.astype(BF16)

    mine_tail, other_tail = tail_of(recv, quarter), tail_of(other, quarter)
    low, high = jnp.where(first, recv, other), jnp.where(first, other, recv)
    low_tail = jnp.where(first, mine_tail, other_tail)
    high_tail = jnp.where(first, other_tail, mine_tail)
    x = jnp.concatenate([low[:, :half], high[:, :half]], axis=1)
    dy = jnp.concatenate(
        [low[:, half : 3 * quarter], low_tail, high[:, half : 3 * quarter], high_tail], axis=1
    )

    gate = dot(x, wg, 1, 0)
    up = dot(x, wu, 1, 0)
    silu_gate = jax.nn.silu(gate)
    hidden = (silu_gate * up).astype(BF16)
    back = dot(dy, wd, 1, 1)
    prob_part = jnp.sum(hidden.astype(F32) * back, axis=1, keepdims=True).astype(BF16)
    d_hidden = weight * back
    sigma = jax.nn.sigmoid(gate)
    d_gate = (d_hidden * up * sigma * (1.0 + gate * (1.0 - sigma))).astype(BF16)
    d_up = (d_hidden * silu_gate).astype(BF16)
    row_part = dot(d_gate, wg, 1, 1) + dot(d_up, wu, 1, 1)

    mine = jnp.where(first, row_part[:, :half], row_part[:, half:])
    yours = jnp.where(first, row_part[:, half:], row_part[:, :half]).astype(BF16)
    swapped = lax.ppermute(
        jnp.concatenate([yours, jnp.broadcast_to(prob_part, (slots, 128))], axis=1), "tp", SWAP
    )
    d_row = (mine + swapped[:, :half].astype(F32)).astype(BF16)
    prob = (prob_part.astype(F32) + swapped[:, half:].astype(F32)).astype(BF16)
    size = half // 4
    is_slot = iota((slots, 1), 0) % ROWS < CAP
    tail = d_row[:, 3 * size :]
    pieces = []
    for j in range(3):
        here = (row_i == j) & (slot_i == CAP) | (row_i == 3 + j) & (slot_i == CAP + 1)
        moved = dot((same & here).astype(BF16), tail, 1, 0).astype(BF16)
        pieces.append(jnp.where(is_slot, d_row[:, j * size : (j + 1) * size], moved))
    back_sent = jnp.concatenate(pieces + [prob], axis=1).reshape(groups, ROWS, 3 * size + 128)

    back_sent, hidden, d_gate, d_up = lax.optimization_barrier((back_sent, hidden, d_gate, d_up))
    back_recv = lax.all_to_all(back_sent, "expert", split_axis=0, concat_axis=0, tiled=True)
    back_recv = back_recv.reshape(slots, 3 * size + 128)

    grads = replica_sum(low, high, low_tail, high_tail, d_gate, d_up, hidden)
    grad_gate, grad_up = grads[:, :hidden_units], grads[:, hidden_units : 2 * hidden_units]
    grad_down = grads[:, 2 * hidden_units :].T

    summed = dot(head_map, back_recv[:, : 3 * size], 1, 0)
    summed_tail = 0.0
    for j in range(3):
        summed_tail += dot(tail_maps[j], back_recv[:, j * size : (j + 1) * size], 1, 0)
    summed = jnp.concatenate([summed, summed_tail], axis=1).astype(BF16)
    summed_other = lax.ppermute(summed, "tp", SWAP)
    d_tokens = jnp.where(
        first,
        jnp.concatenate([summed, summed_other], axis=1),
        jnp.concatenate([summed_other, summed], axis=1),
    )
    d_probs = dot(placed.astype(BF16), back_recv[:, 3 * size :], 1, 0)[:, 0]
    d_probs = d_probs.reshape(toks, top).astype(BF16)
    return (d_tokens, d_probs, grad_gate[None], grad_up[None], grad_down[None])


def solution(mesh):
    return jax.shard_map(
        local,
        mesh=mesh,
        in_specs=(
            P(("dp", "expert"), None),
            P(("dp", "expert"), None),
            P(("dp", "expert"), None),
            P(("dp", "expert"), None),
            P("expert", None, "tp"),
            P("expert", None, "tp"),
            P("expert", "tp", None),
        ),
        out_specs=(
            P(("dp", "expert"), None),
            P(("dp", "expert"), None),
            P("expert", "dp", "tp"),
            P("expert", "dp", "tp"),
            P("expert", "tp", "dp"),
        ),
        check_vma=False,
    )
```
